1024 devices in a mesh: gx: 16 (over x, z_hi), gy: 8 (over z_lo, core), gz: 8 (over y).
Axes of the slice: x: 8, y: 8, z: 8 (z_hi: 2, z_lo: 4; z = z_hi * 4 + z_lo), core: 2. Of those that a mesh axis runs over, the one named last changes fastest.
Arguments:
- body_pos: float32 [3, 524288], P(None, ('gx', 'gy', 'gz')), may hold values from -1 to 1
- body_mass: float32 [524288], P(('gx', 'gy', 'gz')), may hold values from 0.003 to 0.03
- cell_mass: float32 [2097152], P(('gx', 'gy', 'gz')), may hold values from 0.003 to 0.03
- cell_center: float32 [3, 2097152], P(None, ('gx', 'gy', 'gz')), may hold values from -1 to 1
- cell_quad: float32 [6, 2097152], P(None, ('gx', 'gy', 'gz')), may hold values from -0.001 to 0.001
- cell_lists: int32 [1024, 5, 1024], P(('gx', 'gy', 'gz')), may hold values from 0 to 6143, as said below
- slot_masks: int32 [1024, 5, 1024], P(('gx', 'gy', 'gz')), may hold values from 0 to 1, as said below
- face_lists: int32 [1024, 2, 4], P(('gx', 'gy', 'gz')), may hold values from 0 to 3, as said below
- face_counts: int32 [1024, 2], P(('gx', 'gy', 'gz')), may hold values from 1 to 4
Outputs:
- accel: float32 [3, 524288], P(None, ('gx', 'gy', 'gz'))
The draws below stay inside these ranges and needn't reach their ends.
Inputs may be any that keep to these rules, and one draw needn't show every extreme that they name: `cell_lists`: at level l (from 0) every entry is below 2048 + l * 1024, and the 1024 entries of one level of one domain are distinct. `slot_masks`: each level of each domain has exactly 768 ones. `face_lists`: each side's list of a domain is a permutation of its 4 blocks.
All inputs are finite; a program needn't handle non-finite values.
Results may differ from the reference program's by a relative error of at most 0.00002.
Values sent between devices are 32-bit elements; how exact they have to be, the bound alone decides.
A program may use at most 64 MiB of HBM per device.

```python
import math
import jax
import jax.numpy as jnp
from jax import lax

CELLS = 2048
K = 1024
KV = 768
NBLK = 4
BLK = 128
LEVELS = 5
DOMAINS = 1024
ZDOMAINS = 8
BOD = 512
NBODY = 524288
NCELL = 2097152


def draw_cell_lists(key, part):
    span = CELLS + (LEVELS - 1) * K
    spread = 2 ** 30 // span
    positions = jnp.arange(span).astype(jnp.int32)

    def one_device(device_key):

        def one_level(level_no):
            level_key = jax.random.fold_in(device_key, level_no)
            limit = CELLS + level_no * K
            scores = jax.random.randint(level_key, (span,), 0, spread) * span + positions
            scores = jnp.where(positions < limit, scores, 2 ** 30 + positions)
            return jnp.argsort(scores, stable=True)[:K].astype(jnp.int32)
        return lax.map(one_level, jnp.arange(LEVELS).astype(jnp.int32))
    device_keys = jax.random.split(jax.random.fold_in(key, 11), DOMAINS)
    return lax.map(one_device, device_keys)


def draw_slot_masks(key, part):
    slot_keys = jax.random.split(jax.random.fold_in(key, 23), DOMAINS * LEVELS)
    orders = jax.vmap(lambda one_key: jax.random.permutation(one_key, K))(slot_keys)
    return (orders < KV).astype(jnp.int32).reshape(DOMAINS, LEVELS, K)


def draw_face_lists(key, part):
    side_keys = jax.random.split(jax.random.fold_in(key, 37), DOMAINS * 2)
    orders = jax.vmap(lambda one_key: jax.random.permutation(one_key, NBLK))(side_keys)
    return orders.astype(jnp.int32).reshape(DOMAINS, 2, NBLK)


def draw_face_counts(key, part):
    counts = jax.random.randint(jax.random.fold_in(key, 41), (DOMAINS, 2), 1, NBLK + 1)
    counts = counts.at[0, 0].set(NBLK)
    counts = counts.at[1, 1].set(1)
    return counts.astype(jnp.int32)


def block_scale(rng, shape, shards, low, top_value):
    factor_of, own = 1.0, jax.random.fold_in(rng, 6)
    for axis_at, shards_of in shards:
        heights = jnp.exp(jax.random.uniform(jax.random.fold_in(own, axis_at), (shards_of,), jnp.float32, low / len(shards), top_value / len(shards)))
        factor_of = factor_of * jnp.repeat(heights, shape[axis_at] // shards_of).reshape([-1 if axis == axis_at else 1 for axis in range(len(shape))])
    return factor_of


def setup_inputs(seed: int = 0) -> dict:
    arg_keys = jax.random.split(jax.random.key(seed), 10)
    body_pos = jnp.clip(jax.random.uniform(arg_keys[0], (3, NBODY), jnp.float32, -1.0, 1.0) * block_scale(arg_keys[0], (3, NBODY), ((1, 1024),), -0.4, 0.0), -1.0, 1.0)
    body_mass = jnp.clip(jnp.exp(math.log(0.03) - 2.3025851 * jax.random.uniform(arg_keys[1], (NBODY,), jnp.float32) ** block_scale(arg_keys[1], (NBODY,), ((0, 1024),), -0.2, 0.2)), 0.003, 0.03)
    cell_mass = jnp.clip(jnp.exp(math.log(0.03) - 2.3025851 * jax.random.uniform(arg_keys[2], (NCELL,), jnp.float32) ** block_scale(arg_keys[2], (NCELL,), ((0, 1024),), -0.2, 0.2)), 0.003, 0.03)
    cell_center = jnp.clip(jax.random.uniform(arg_keys[3], (3, NCELL), jnp.float32, -1.0, 1.0) * block_scale(arg_keys[3], (3, NCELL), ((1, 1024),), -0.4, 0.0), -1.0, 1.0)
    cell_quad = jnp.clip(jax.random.uniform(arg_keys[4], (6, NCELL), jnp.float32, -0.001, 0.001) * block_scale(arg_keys[4], (6, NCELL), ((1, 1024),), -0.4, 0.0), -0.001, 0.001)
    cell_lists = draw_cell_lists(jax.random.fold_in(arg_keys[9], 71), 0)
    slot_masks = draw_slot_masks(jax.random.fold_in(arg_keys[9], 71), 0)
    face_lists = draw_face_lists(jax.random.fold_in(arg_keys[9], 71), 0)
    face_counts = draw_face_counts(jax.random.fold_in(arg_keys[9], 71), 0)
    return dict(body_pos=body_pos, body_mass=body_mass, cell_mass=cell_mass, cell_center=cell_center, cell_quad=cell_quad, cell_lists=cell_lists, slot_masks=slot_masks, face_lists=face_lists, face_counts=face_counts)


soften = 0.01

def tile_accel(targets, sources):
    offset = targets[:, :, None] - sources[1:4, None, :]
    distance = lax.optimization_barrier(jnp.sum(offset * offset, axis=0)) + soften
    inverse_one = lax.rsqrt(distance)
    inverse_two = inverse_one * inverse_one
    inverse_three = inverse_one * inverse_two
    radial = -sources[0][None, :] * inverse_three
    if sources.shape[0] == 10:
        quadrupole = sources[4:10]
        quad_x = quadrupole[0][None, :] * offset[0] + quadrupole[3][None, :] * offset[1] + quadrupole[4][None, :] * offset[2]
        quad_y = quadrupole[3][None, :] * offset[0] + quadrupole[1][None, :] * offset[1] + quadrupole[5][None, :] * offset[2]
        quad_z = quadrupole[4][None, :] * offset[0] + quadrupole[5][None, :] * offset[1] + quadrupole[2][None, :] * offset[2]
        inverse_five = inverse_three * inverse_two
        quad_form = offset[0] * quad_x + offset[1] * quad_y + offset[2] * quad_z
        radial = radial - 2.5 * quad_form * inverse_five * inverse_two
        return jnp.stack([lax.optimization_barrier(jnp.sum(radial * offset[0] + quad_x * inverse_five, axis=1)), lax.optimization_barrier(jnp.sum(radial * offset[1] + quad_y * inverse_five, axis=1)), lax.optimization_barrier(jnp.sum(radial * offset[2] + quad_z * inverse_five, axis=1))])
    return lax.optimization_barrier(jnp.sum(radial[None] * offset, axis=2))

def domain_accel(inputs):
    targets, held_cells, near_bodies = inputs
    return tile_accel(targets, held_cells) + tile_accel(targets, near_bodies)

def reference(body_pos, body_mass, cell_mass, cell_center, cell_quad, cell_lists, slot_masks, face_lists, face_counts):
    bit_count = DOMAINS.bit_length() - 1
    domain_ids = jnp.arange(DOMAINS).astype(jnp.int32)
    own_cells = jnp.concatenate([cell_mass[None], cell_center, cell_quad], 0)
    held_cells = own_cells.reshape(10, DOMAINS, CELLS).transpose(1, 0, 2)
    for level_no in range(LEVELS):
        partner = domain_ids ^ 1 << bit_count - 1 - level_no
        picked = jax.vmap(lambda cells_held, slot_index: jnp.take(cells_held, slot_index, axis=1))(held_cells, cell_lists[:, level_no, :])
        picked = picked * slot_masks[:, level_no, None, :].astype(picked.dtype)
        held_cells = jnp.concatenate([held_cells, picked[partner]], axis=2)
    bodies = jnp.concatenate([body_mass[None], body_pos], 0).reshape(4, DOMAINS, NBLK, BLK).transpose(1, 0, 2, 3)
    selected = jax.vmap(lambda blocks, block_index: jnp.take(blocks, block_index, axis=1))(bodies, face_lists.reshape(DOMAINS, 2 * NBLK))
    live_slots = jnp.arange(NBLK).astype(jnp.int32)[None, None, :] < face_counts[:, :, None]
    selected = selected * live_slots.reshape(DOMAINS, 1, 2 * NBLK, 1).astype(selected.dtype)
    selected = selected.reshape(DOMAINS, 4, 2, NBLK * BLK)
    z_index = domain_ids % ZDOMAINS
    lower_ids = jnp.maximum(domain_ids - 1, 0)
    upper_ids = jnp.minimum(domain_ids + 1, DOMAINS - 1)
    from_lower = jnp.where((z_index > 0)[:, None, None], selected[lower_ids][:, :, 1, :], 0.0)
    from_upper = jnp.where((z_index < ZDOMAINS - 1)[:, None, None], selected[upper_ids][:, :, 0, :], 0.0)
    near_bodies = jnp.concatenate([bodies.reshape(DOMAINS, 4, BOD), from_lower, from_upper], axis=2)
    targets = body_pos.reshape(3, DOMAINS, BOD).transpose(1, 0, 2)
    accelerations = lax.map(domain_accel, (targets, held_cells, near_bodies))
    return accelerations.transpose(1, 0, 2).reshape(3, DOMAINS * BOD)
```

```python
import functools

import jax
import jax.numpy as jnp
from jax import lax
from jax.experimental import pallas as pl
from jax.experimental.pallas import tpu as pltpu
from jax.sharding import PartitionSpec as P

MESH = pl.DeviceIdType.MESH
AXES = ("gx", "gy", "gz")
SOFTEN = 0.01
LANES = 128
OWN = 2048 // LANES
SLOTS = 1024 // LANES
LIVE = 768 // LANES
GROUP = 32
KEEP = 8192


def row8(row):
    return jnp.broadcast_to(row, (8, LANES))


def flipped(value, bit):
    unit = 2**bit
    return value + unit - 2 * unit * lax.rem(lax.div(value, unit), 2)


def kernel(
    sizes,
    levels,
    pos_h,
    mass_h,
    cm_h,
    cc_h,
    cq_h,
    lists_h,
    masks_h,
    face_lists,
    face_counts,
    out_ref,
    pos,
    mass,
    cm,
    cc,
    cq,
    lists,
    masks,
    xb,
    acc,
    slot_ids,
    ranks,
    their_ranks,
    part,
    sent,
    got,
    bodies_out,
    bodies_in,
    in_sem,
    send_sem,
    recv_sem,
    rank_send_sem,
    rank_recv_sem,
    body_send_sem,
    body_recv_sem,
):
    nx, ny, nz = sizes
    bz, by = nz.bit_length() - 1, ny.bit_length() - 1
    bits = nx.bit_length() - 1 + by + bz
    gx, gy, gz = (lax.axis_index(a) for a in AXES)

    loads = {}
    for n, (name, src, dst) in enumerate(
        (
            ("lists", lists_h, lists),
            ("masks", masks_h, masks),
            ("cm", cm_h, cm),
            ("cc", cc_h, cc),
            ("cq", cq_h, cq),
            ("pos", pos_h, pos),
            ("mass", mass_h, mass),
        )
    ):
        loads[name] = pltpu.make_async_copy(src, dst, in_sem.at[n])
        loads[name].start()

    partners = []
    for level in range(levels):
        bit = bits - 1 - level
        if bit >= by + bz:
            partners.append((flipped(gx, bit - by - bz), gy, gz))
        elif bit >= bz:
            partners.append((gx, flipped(gy, bit - bz), gz))
        else:
            partners.append((gx, gy, flipped(gz, bit)))
    lower = (gx, gy, lax.rem(gz + nz - 1, nz))
    upper = (gx, gy, lax.rem(gz + 1, nz))
    barrier = pltpu.get_barrier_semaphore()
    for peer in partners + [lower, upper]:
        pl.semaphore_signal(barrier, inc=1, device_id=peer, device_id_type=MESH)

    loads["lists"].wait()
    loads["masks"].wait()
    lane = lax.broadcasted_iota(jnp.int32, (8, LANES), 1)

    def chunk8(ref, q):
        rows = ref[0, :, q * LANES : (q + 1) * LANES]
        pad = jnp.zeros((8 - levels, LANES), jnp.int32)
        return jnp.concatenate([rows, pad], axis=0) if levels < 8 else rows

    live = [chunk8(masks, q) for q in range(SLOTS)]
    stacked = jnp.concatenate(live, axis=0).astype(jnp.float32)
    earlier = (
        lax.broadcasted_iota(jnp.int32, (LANES, LANES), 0)
        < lax.broadcasted_iota(jnp.int32, (LANES, LANES), 1)
    ).astype(jnp.float32)
    before = jnp.dot(stacked, earlier, preferred_element_type=jnp.float32)
    totals = jnp.dot(
        stacked, jnp.ones((LANES, LANES), jnp.float32), preferred_element_type=jnp.float32
    )
    base = jnp.zeros((8, LANES), jnp.float32)
    packed = []
    for q in range(SLOTS):
        rank = (before[8 * q : 8 * q + 8] + base).astype(jnp.int32)
        base = base + totals[8 * q : 8 * q + 8]
        on = live[q] > 0
        where = jnp.where(on, rank, -1)
        for level in range(levels - 1):
            ranks[level, q : q + 1, :] = where[level : level + 1]
        moves = lane + q * LANES - rank
        packed.append(jnp.where(on, chunk8(lists, q) + moves * KEEP, 0))
    shift = 1
    while shift <= (SLOTS - LIVE) * LANES:
        flag = shift * KEEP
        if shift < LANES:
            turned = [pltpu.roll(w, LANES - shift, 1) for w in packed] + [jnp.zeros((8, LANES), jnp.int32)]
            coming = [
                jnp.where(lane < LANES - shift, turned[q], turned[q + 1]) for q in range(SLOTS)
            ]
        else:
            step = shift // LANES
            coming = [
                packed[q + step] if q + step < SLOTS else jnp.zeros((8, LANES), jnp.int32)
                for q in range(SLOTS)
            ]
        packed = [
            jnp.where((c & flag) != 0, c, jnp.where((w & flag) != 0, 0, w))
            for c, w in zip(coming, packed)
        ]
        shift *= 2
    for q in range(LIVE):
        slots = packed[q] & (KEEP - 1)
        for level in range(levels):
            slot_ids[level, q : q + 1, :] = slots[level : level + 1]
    for level in range(levels):
        slot_ids[level, LIVE:, :] = jnp.full((8 - LIVE, LANES), -1, jnp.int32)

    def own_row(c, k):
        if c == 0:
            return cm[pl.ds(k, 1), :]
        ref, r = (cc, c - 1) if c < 4 else (cq, c - 4)
        if isinstance(k, int):
            return ref[r : r + 1, k * LANES : (k + 1) * LANES]
        return ref[r : r + 1, pl.ds(pl.multiple_of(k * LANES, LANES), LANES)]

    def got_row(level):
        return lambda c, k: got[level, c * LIVE + k : c * LIVE + k + 1, :]

    def pick_own(level):
        ids = slot_ids[level]
        rows, cols = ids >> 7, ids & (LANES - 1)

        def step(k, found):
            here = rows == k
            return tuple(
                jnp.where(here, jnp.take_along_axis(row8(own_row(c, k)), cols, axis=1), found[c])
                for c in range(10)
            )

        found = tuple(jnp.zeros((8, LANES), jnp.float32) for _ in range(10))
        found = lax.fori_loop(0, OWN, step, found, unroll=8)
        return list(found)

    def pick_got(level, source, found):
        ids = slot_ids[level]
        rows, cols = ids >> 7, ids & (LANES - 1)
        for k in range(LIVE):
            here = rows == OWN + source * SLOTS + k
            for c in range(10):
                row = row8(got_row(source)(c, k))
                found[c] = jnp.where(here, jnp.take_along_axis(row, cols, axis=1), found[c])
        return found

    def translate(level, source):
        ids = slot_ids[level]
        rows, cols = ids >> 7, ids & (LANES - 1)
        first = OWN + source * SLOTS
        place = ids
        for k in range(SLOTS):
            row = row8(their_ranks[source, k : k + 1, :])
            value = jnp.take_along_axis(row, cols, axis=1)
            value = jnp.where(value < 0, -1, value + first * LANES)
            place = jnp.where(rows == first + k, value, place)
        slot_ids[level] = place

    def send(level, found):
        for c in range(10):
            sent[level, c * LIVE : (c + 1) * LIVE, :] = found[c][:LIVE]
        copies[level].start()

    copies = [
        pltpu.make_async_remote_copy(
            src_ref=sent.at[level],
            dst_ref=got.at[level],
            send_sem=send_sem.at[level],
            recv_sem=recv_sem.at[level],
            device_id=partners[level],
            device_id_type=MESH,
        )
        for level in range(levels)
    ]
    rank_copies = [
        pltpu.make_async_remote_copy(
            src_ref=ranks.at[level],
            dst_ref=their_ranks.at[level],
            send_sem=rank_send_sem.at[level],
            recv_sem=rank_recv_sem.at[level],
            device_id=partners[level],
            device_id_type=MESH,
        )
        for level in range(levels - 1)
    ]
    body_copies = [
        pltpu.make_async_remote_copy(
            src_ref=bodies_out.at[side],
            dst_ref=bodies_in.at[1 - side],
            send_sem=body_send_sem.at[side],
            recv_sem=body_recv_sem.at[1 - side],
            device_id=peer,
            device_id_type=MESH,
        )
        for side, peer in enumerate((lower, upper))
    ]

    loads["cm"].wait()
    loads["cc"].wait()
    loads["cq"].wait()
    found = pick_own(0)
    for c in range(10):
        sent[0, c * LIVE : (c + 1) * LIVE, :] = found[c][:LIVE]
    loads["pos"].wait()
    loads["mass"].wait()
    for side in range(2):
        for block in range(4):
            listed = jnp.int32(0)
            for j in range(4):
                hit = (face_lists[0, side, j] == block) & (j < face_counts[0, side])
                listed = listed + hit.astype(jnp.int32)
            kept = jnp.where(listed > 0, mass[block : block + 1, :], 0.0)
            bodies_out[side, block : block + 1, :] = kept
        for a in range(3):
            for block in range(4):
                bodies_out[side, 4 + 4 * a + block : 5 + 4 * a + block, :] = pos[
                    a : a + 1, block * LANES : (block + 1) * LANES
                ]

    pl.semaphore_wait(barrier, levels + 2)
    copies[0].start()
    for copy in rank_copies + body_copies:
        copy.start()

    for a in range(3):
        for block in range(4):
            row = pos[a : a + 1, block * LANES : (block + 1) * LANES]
            xb[a, block * LANES : (block + 1) * LANES, :] = jnp.broadcast_to(
                row, (LANES, LANES)
            ).T
    acc[...] = jnp.zeros_like(acc)

    def add_cells(read, rows, first, count):
        def step(g, _):
            at = pl.multiple_of(first + g * GROUP, GROUP)
            x = [xb[a, pl.ds(at, GROUP), :] for a in range(3)]
            total = [acc[a, pl.ds(at, GROUP), :] for a in range(3)]
            for k in rows:
                m, c0, c1, c2, xx, yy, zz, xy, xz, yz = (read(c, k) for c in range(10))
                d0, d1, d2 = x[0] - c0, x[1] - c1, x[2] - c2
                s = (d0 * d0 + d1 * d1) + (d2 * d2 + SOFTEN)
                u = lax.rsqrt(s)
                u2 = u * u
                q0 = xx * d0 + xy * d1 + xz * d2
                q1 = xy * d0 + yy * d1 + yz * d2
                q2 = xz * d0 + yz * d1 + zz * d2
                form = d0 * q0 + d1 * q1 + d2 * q2
                u5 = u2 * u2 * u
                w = m * s + 2.5 * (form * u2)
                total[0] = total[0] + u5 * (q0 - w * d0)
                total[1] = total[1] + u5 * (q1 - w * d1)
                total[2] = total[2] + u5 * (q2 - w * d2)
            for a in range(3):
                acc[a, pl.ds(at, GROUP), :] = total[a]
            return 0

        lax.fori_loop(0, count // GROUP, step, 0)

    def add_bodies(read, rows):
        def step(g, _):
            at = pl.multiple_of(g * GROUP, GROUP)
            x = [xb[a, pl.ds(at, GROUP), :] for a in range(3)]
            total = [acc[a, pl.ds(at, GROUP), :] for a in range(3)]
            for k in rows:
                m, c0, c1, c2 = (read(c, k) for c in range(4))
                d0, d1, d2 = x[0] - c0, x[1] - c1, x[2] - c2
                s = (d0 * d0 + d1 * d1) + (d2 * d2 + SOFTEN)
                u = lax.rsqrt(s)
                p = m * (u * u * u)
                total[0] = total[0] - p * d0
                total[1] = total[1] - p * d1
                total[2] = total[2] - p * d2
            for a in range(3):
                acc[a, pl.ds(at, GROUP), :] = total[a]
            return 0

        lax.fori_loop(0, 512 // GROUP, step, 0)

    def own(lo, hi):
        add_cells(own_row, range(lo, hi), 0, 512)

    def arrived(level):
        add_cells(got_row(level), range(LIVE), 0, 512)

    def own_bodies(c, k):
        if c == 0:
            return mass[k : k + 1, :]
        return pos[c - 1 : c, k * LANES : (k + 1) * LANES]

    def near(side):
        body_copies[1 - side].wait_recv()
        inside = (gz > 0) if side == 0 else (gz < nz - 1)

        @pl.when(inside)
        def _():
            add_bodies(lambda c, k: bodies_in[side, 4 * c + k : 4 * c + k + 1, :], range(4))

    def keep(level, found):
        for c in range(10):
            part[level, c] = found[c]

    def kept(level):
        return [part[level, c] for c in range(10)]

    for level in range(1, levels):
        keep(level, pick_own(level))
    work = [
        [lambda: own(0, 6), lambda: own(6, 12)],
        [lambda: add_bodies(own_bodies, range(4)), lambda: own(12, 16)],
        [lambda: near(0), lambda: near(1), lambda: arrived(0)],
        [lambda: arrived(1), lambda: arrived(2)],
        [lambda: arrived(3)],
    ]
    for level in range(levels):
        for job in work[level]:
            job()
        if level < levels - 1:
            rank_copies[level].wait_recv()
            for later in range(level + 1, levels):
                translate(later, level)
            copies[level].wait_recv()
            send(level + 1, pick_got(level + 1, level, kept(level + 1)))
            for later in range(level + 2, levels):
                keep(later, pick_got(later, level, kept(later)))
        else:
            copies[level].wait_recv()
    for block in range(4):
        add_cells(got_row(levels - 1), range(LIVE), block * LANES, LANES)
        for a in range(3):
            turned = acc[a, block * LANES : (block + 1) * LANES, :].T
            out_ref[a : a + 1, block * LANES : (block + 1) * LANES] = jnp.sum(
                turned, axis=0, keepdims=True
            )
    for copy in copies + rank_copies + body_copies:
        copy.wait_send()


def shards(sizes, pos, mass, cm, cc, cq, lists, masks, face_lists, face_counts):
    levels = lists.shape[1]
    f32, i32 = jnp.float32, jnp.int32
    any_space = pl.BlockSpec(memory_space=pl.ANY)
    smem = pl.BlockSpec(memory_space=pltpu.SMEM)
    dma = pltpu.SemaphoreType.DMA
    return pl.pallas_call(
        functools.partial(kernel, sizes, levels),
        out_shape=jax.ShapeDtypeStruct(pos.shape, f32),
        in_specs=[any_space] * 7 + [smem] * 2,
        out_specs=pl.BlockSpec(memory_space=pltpu.VMEM),
        scratch_shapes=[
            pltpu.VMEM(pos.shape, f32),
            pltpu.VMEM((4, LANES), f32),
            pltpu.VMEM((OWN, LANES), f32),
            pltpu.VMEM(cc.shape, f32),
            pltpu.VMEM(cq.shape, f32),
            pltpu.VMEM(lists.shape, i32),
            pltpu.VMEM(masks.shape, i32),
            pltpu.VMEM((3, 512, LANES), f32),
            pltpu.VMEM((3, 512, LANES), f32),
            pltpu.VMEM((levels, 8, LANES), i32),
            pltpu.VMEM((levels - 1, SLOTS, LANES), i32),
            pltpu.VMEM((levels - 1, SLOTS, LANES), i32),
            pltpu.VMEM((levels, 10, 8, LANES), f32),
            pltpu.VMEM((levels, 10 * LIVE, LANES), f32),
            pltpu.VMEM((levels, 10 * LIVE, LANES), f32),
            pltpu.VMEM((2, 16, LANES), f32),
            pltpu.VMEM((2, 16, LANES), f32),
            dma((7,)),
            dma((levels,)),
            dma((levels,)),
            dma((levels - 1,)),
            dma((levels - 1,)),
            dma((2,)),
            dma((2,)),
        ],
        compiler_params=pltpu.CompilerParams(collective_id=0, has_side_effects=True),
        name="treecode",
    )(
        pos,
        mass.reshape(4, LANES),
        cm.reshape(OWN, LANES),
        cc,
        cq,
        lists,
        masks,
        face_lists,
        face_counts,
    )


def solution(mesh):
    sizes = tuple(mesh.shape[a] for a in AXES)
    in_specs = (
        P(None, AXES),
        P(AXES),
        P(AXES),
        P(None, AXES),
        P(None, AXES),
        P(AXES, None, None),
        P(AXES, None, None),
        P(AXES, None, None),
        P(AXES, None),
    )
    return jax.shard_map(
        functools.partial(shards, sizes),
        mesh=mesh,
        in_specs=in_specs,
        out_specs=P(None, AXES),
        check_vma=False,
    )
```

```python
import functools

import jax
import jax.numpy as jnp
from jax import lax
from jax.experimental import pallas as pl
from jax.experimental.pallas import tpu as pltpu
from jax.sharding import PartitionSpec as P

MESH = pl.DeviceIdType.MESH
AXES = ("gx", "gy", "gz")
SOFTEN = 0.01
LANES = 128
OWN = 2048 // LANES
SLOTS = 1024 // LANES
LIVE = 768 // LANES
COMPS = 10
BLOCK = 64
GROUP = 32
KEEP = 8192
PLAN = (
    (8, 7, 2, 0),
    (8, 8, 3, 1),
    (9, 10, 5, 3),
    (11, 11, 7, 5),
    (15, 13, 9, 7),
    (20, 20, 12, 10),
)


def row8(row):
    return jnp.broadcast_to(row, (8, LANES))


def flipped(value, bit):
    unit = 2**bit
    return value + unit - 2 * unit * lax.rem(lax.div(value, unit), 2)


def kernel(
    sizes,
    levels,
    pos_h,
    mass_h,
    cm_h,
    cc_h,
    cq_h,
    lists_h,
    masks_h,
    face_lists,
    face_counts,
    out_ref,
    pos,
    mass,
    cm,
    cc,
    cq,
    lists,
    masks,
    xb,
    acc,
    slot_ids,
    ranks,
    their_ranks,
    part,
    sent,
    table,
    bodies_out,
    bodies_in,
    in_sem,
    send_sem,
    recv_sem,
    rank_send_sem,
    rank_recv_sem,
    body_send_sem,
    body_recv_sem,
):
    nx, ny, nz = sizes
    bz, by = nz.bit_length() - 1, ny.bit_length() - 1
    bits = nx.bit_length() - 1 + by + bz
    gx, gy, gz = (lax.axis_index(a) for a in AXES)

    loads = {}
    for n, (name, src, dst) in enumerate(
        (
            ("lists", lists_h, lists),
            ("masks", masks_h, masks),
            ("cm", cm_h, cm),
            ("cc", cc_h, cc),
            ("cq", cq_h, cq),
            ("pos", pos_h, pos),
            ("mass", mass_h, mass),
        )
    ):
        loads[name] = pltpu.make_async_copy(src, dst, in_sem.at[n])
        loads[name].start()

    partners = []
    for level in range(levels):
        bit = bits - 1 - level
        if bit >= by + bz:
            partners.append((flipped(gx, bit - by - bz), gy, gz))
        elif bit >= bz:
            partners.append((gx, flipped(gy, bit - bz), gz))
        else:
            partners.append((gx, gy, flipped(gz, bit)))
    lower = (gx, gy, lax.rem(gz + nz - 1, nz))
    upper = (gx, gy, lax.rem(gz + 1, nz))
    barrier = pltpu.get_barrier_semaphore()
    for peer in partners + [lower, upper]:
        pl.semaphore_signal(barrier, inc=1, device_id=peer, device_id_type=MESH)

    late = lax.rem(gx, 2) * 2 + lax.div(gy, 4)
    others = lax.div((gx * ny + gy) * nz + gz + nx * ny * nz - 1, nx * ny * nz)
    late = late + 3 * (1 - others)
    steps = [lax.div(late + 3, 4), lax.div(late + 2, 4), lax.div(late + 1, 4)]

    def bound(window):
        b = PLAN[window]
        return b[0] + sum((b[i + 1] - b[i]) * steps[i] for i in range(3))

    loads["lists"].wait()
    loads["masks"].wait()
    lane = lax.broadcasted_iota(jnp.int32, (8, LANES), 1)
    slot = lax.broadcasted_iota(jnp.int32, (8, LANES), 0) * LANES + lane

    def dot(x, y):
        return jnp.dot(x, y, preferred_element_type=jnp.float32)

    def square(n, test):
        i = lax.broadcasted_iota(jnp.int32, (n, n), 0)
        j = lax.broadcasted_iota(jnp.int32, (n, n), 1)
        return test(i, j).astype(jnp.float32)

    stacked = jnp.concatenate([masks[level] for level in range(levels)], axis=0)
    stacked = stacked.astype(jnp.float32)
    before = dot(stacked, square(LANES, lambda i, j: i < j))
    totals = dot(stacked, jnp.ones((LANES, LANES), jnp.float32))
    base = dot(square(8 * levels, lambda i, j: ((i >> 3) == (j >> 3)) & (i > j)), totals)
    rank = (before + base).astype(jnp.int32)
    packed = []
    for level in range(levels):
        place = rank[8 * level : 8 * level + 8]
        on = masks[level] > 0
        if level < levels - 1:
            ranks[level] = jnp.where(on, place, -1)
        packed.append(jnp.where(on, lists[level] + (slot - place) * KEEP, 0))
    shift = 1
    while shift <= (SLOTS - LIVE) * LANES:
        flag = shift * KEEP
        for level in range(levels):
            w = packed[level]
            if shift < LANES:
                turned = pltpu.roll(w, LANES - shift, 1)
                coming = jnp.where(lane < LANES - shift, turned, pltpu.roll(turned, 7, 0))
            else:
                coming = pltpu.roll(w, 8 - shift // LANES, 0)
            coming = jnp.where(slot < SLOTS * LANES - shift, coming, 0)
            stay = jnp.where((w & flag) != 0, 0, w)
            packed[level] = jnp.where((coming & flag) != 0, coming, stay)
        shift *= 2
    for level in range(levels):
        slot_ids[level] = jnp.where(slot < LIVE * LANES, packed[level] & (KEEP - 1), -1)

    def level_start(level):
        return OWN * COMPS + BLOCK * level

    def own_row(c, k):
        return table[pl.ds(k * COMPS + c, 1), :]

    def got_row(level):
        return lambda c, k: table[pl.ds(level_start(level) + k * COMPS + c, 1), :]

    def pick_own(level):
        ids = slot_ids[level]
        rows, cols = ids >> 7, ids & (LANES - 1)

        def step(k, found):
            here = rows == k
            return tuple(
                jnp.where(here, jnp.take_along_axis(row8(own_row(c, k)), cols, axis=1), found[c])
                for c in range(10)
            )

        found = tuple(jnp.zeros((8, LANES), jnp.float32) for _ in range(10))
        found = lax.fori_loop(0, OWN, step, found, unroll=8)
        return list(found)

    def pick_got(level, source, found):
        ids = slot_ids[level]
        rows, cols = ids >> 7, ids & (LANES - 1)
        for k in range(LIVE):
            here = rows == OWN + source * SLOTS + k
            for c in range(10):
                row = row8(got_row(source)(c, k))
                found[c] = jnp.where(here, jnp.take_along_axis(row, cols, axis=1), found[c])
        return found

    def translate(level, source):
        ids = slot_ids[level]
        rows, cols = ids >> 7, ids & (LANES - 1)
        first = OWN + source * SLOTS
        place = ids
        for k in range(SLOTS):
            row = row8(their_ranks[source, k : k + 1, :])
            value = jnp.take_along_axis(row, cols, axis=1)
            value = jnp.where(value < 0, -1, value + first * LANES)
            place = jnp.where(rows == first + k, value, place)
        slot_ids[level] = place

    def stage(level, found):
        for c in range(COMPS):
            sent[level, pl.ds(c, LIVE, stride=COMPS), :] = found[c][:LIVE]

    def send(level, found):
        stage(level, found)
        copies[level].start()

    copies = [
        pltpu.make_async_remote_copy(
            src_ref=sent.at[level],
            dst_ref=table.at[pl.ds(level_start(level), BLOCK)],
            send_sem=send_sem.at[level],
            recv_sem=recv_sem.at[level],
            device_id=partners[level],
            device_id_type=MESH,
        )
        for level in range(levels)
    ]
    rank_copies = [
        pltpu.make_async_remote_copy(
            src_ref=ranks.at[level],
            dst_ref=their_ranks.at[level],
            send_sem=rank_send_sem.at[level],
            recv_sem=rank_recv_sem.at[level],
            device_id=partners[level],
            device_id_type=MESH,
        )
        for level in range(levels - 1)
    ]
    body_copies = [
        pltpu.make_async_remote_copy(
            src_ref=bodies_out.at[side],
            dst_ref=bodies_in.at[1 - side],
            send_sem=body_send_sem.at[side],
            recv_sem=body_recv_sem.at[1 - side],
            device_id=peer,
            device_id_type=MESH,
        )
        for side, peer in enumerate((lower, upper))
    ]

    loads["cm"].wait()
    loads["cc"].wait()
    loads["cq"].wait()
    for k in range(OWN):
        cols = slice(k * LANES, (k + 1) * LANES)
        table[k * COMPS : k * COMPS + 1, :] = cm[k : k + 1, :]
        table[k * COMPS + 1 : k * COMPS + 4, :] = cc[:, cols]
        table[k * COMPS + 4 : (k + 1) * COMPS, :] = cq[:, cols]
    stage(0, pick_own(0))
    loads["pos"].wait()
    loads["mass"].wait()
    for side in range(2):
        for block in range(4):
            listed = jnp.int32(0)
            for j in range(4):
                hit = (face_lists[0, side, j] == block) & (j < face_counts[0, side])
                listed = listed + hit.astype(jnp.int32)
            kept_mass = jnp.where(listed > 0, mass[block : block + 1, :], 0.0)
            bodies_out[side, block : block + 1, :] = kept_mass
        for a in range(3):
            for block in range(4):
                bodies_out[side, 4 + 4 * a + block : 5 + 4 * a + block, :] = pos[
                    a : a + 1, block * LANES : (block + 1) * LANES
                ]

    def spread():
        for a in range(3):
            for block in range(4):
                row = pos[a : a + 1, block * LANES : (block + 1) * LANES]
                xb[a, block * LANES : (block + 1) * LANES, :] = jnp.broadcast_to(
                    row, (LANES, LANES)
                ).T
        acc[...] = jnp.zeros_like(acc)

    def cells_step(read, units, at):
        x = [xb[a, pl.ds(at, GROUP), :] for a in range(3)]
        total = [acc[a, pl.ds(at, GROUP), :] for a in range(3)]
        for k in units:
            m, c0, c1, c2, xx, yy, zz, xy, xz, yz = (read(c, k) for c in range(COMPS))
            d0, d1, d2 = x[0] - c0, x[1] - c1, x[2] - c2
            s = (d0 * d0 + d1 * d1) + (d2 * d2 + SOFTEN)
            u = lax.rsqrt(s)
            u2 = u * u
            q0 = xx * d0 + xy * d1 + xz * d2
            q1 = xy * d0 + yy * d1 + yz * d2
            q2 = xz * d0 + yz * d1 + zz * d2
            form = d0 * q0 + d1 * q1 + d2 * q2
            u5 = u2 * u2 * u
            w = m * s + 2.5 * (form * u2)
            total[0] = total[0] + u5 * (q0 - w * d0)
            total[1] = total[1] + u5 * (q1 - w * d1)
            total[2] = total[2] + u5 * (q2 - w * d2)
        for a in range(3):
            acc[a, pl.ds(at, GROUP), :] = total[a]

    def add_pairs(lo, hi):
        def pair(p, _):
            level = lax.div(jnp.maximum(p - 8, 0), 3)
            start = 2 * COMPS * p + (BLOCK - LIVE * COMPS) * level

            def step(g, _):
                cells_step(
                    lambda c, k: table[pl.ds(start + COMPS * k + c, 1), :],
                    range(2),
                    pl.multiple_of(g * GROUP, GROUP),
                )
                return 0

            return lax.fori_loop(0, 512 // GROUP, step, 0)

        lax.fori_loop(lo, hi, pair, 0)

    def add_bodies(read, rows):
        def step(g, _):
            at = pl.multiple_of(g * GROUP, GROUP)
            x = [xb[a, pl.ds(at, GROUP), :] for a in range(3)]
            total = [acc[a, pl.ds(at, GROUP), :] for a in range(3)]
            for k in rows:
                m, c0, c1, c2 = (read(c, k) for c in range(4))
                d0, d1, d2 = x[0] - c0, x[1] - c1, x[2] - c2
                s = (d0 * d0 + d1 * d1) + (d2 * d2 + SOFTEN)
                u = lax.rsqrt(s)
                p = m * (u * u * u)
                total[0] = total[0] - p * d0
                total[1] = total[1] - p * d1
                total[2] = total[2] - p * d2
            for a in range(3):
                acc[a, pl.ds(at, GROUP), :] = total[a]
            return 0

        lax.fori_loop(0, 512 // GROUP, step, 0)

    def own_bodies(c, k):
        if c == 0:
            return mass[k : k + 1, :]
        return pos[c - 1 : c, k * LANES : (k + 1) * LANES]

    def near(side):
        body_copies[1 - side].wait_recv()
        inside = (gz > 0) if side == 0 else (gz < nz - 1)

        @pl.when(inside)
        def _():
            add_bodies(lambda c, k: bodies_in[side, 4 * c + k : 4 * c + k + 1, :], range(4))

    def keep(level, found):
        for c in range(10):
            part[level, c] = found[c]

    def kept(level):
        return [part[level, c] for c in range(10)]

    early = late < 3

    @pl.when(early)
    def _():
        spread()
        add_pairs(0, bound(0))

    pl.semaphore_wait(barrier, levels + 2)
    copies[0].start()
    for copy in rank_copies + body_copies:
        copy.start()

    @pl.when(jnp.logical_not(early))
    def _():
        spread()

    for level in range(1, levels):
        keep(level, pick_own(level))
    for level in range(levels):
        if level == 3:
            add_bodies(own_bodies, range(4))
            near(0)
            near(1)
        add_pairs(bound(level), bound(level + 1))
        if level < levels - 1:
            rank_copies[level].wait_recv()
            for later in range(level + 1, levels):
                translate(later, level)
        copies[level].wait_recv()
        if level < levels - 1:
            send(level + 1, pick_got(level + 1, level, kept(level + 1)))
            for later in range(level + 2, levels):
                keep(later, pick_got(later, level, kept(later)))
    add_pairs(bound(levels), 8 + 3 * (levels - 1))
    for block in range(4):
        for g in range(LANES // GROUP):
            cells_step(got_row(levels - 1), range(LIVE), block * LANES + g * GROUP)
        for a in range(3):
            turned = acc[a, block * LANES : (block + 1) * LANES, :].T
            out_ref[a : a + 1, block * LANES : (block + 1) * LANES] = jnp.sum(
                turned, axis=0, keepdims=True
            )
    for copy in copies + rank_copies + body_copies:
        copy.wait_send()


def shards(sizes, pos, mass, cm, cc, cq, lists, masks, face_lists, face_counts):
    levels = lists.shape[1]
    f32, i32 = jnp.float32, jnp.int32
    any_space = pl.BlockSpec(memory_space=pl.ANY)
    smem = pl.BlockSpec(memory_space=pltpu.SMEM)
    dma = pltpu.SemaphoreType.DMA
    return pl.pallas_call(
        functools.partial(kernel, sizes, levels),
        out_shape=jax.ShapeDtypeStruct(pos.shape, f32),
        in_specs=[any_space] * 7 + [smem] * 2,
        out_specs=pl.BlockSpec(memory_space=pltpu.VMEM),
        scratch_shapes=[
            pltpu.VMEM(pos.shape, f32),
            pltpu.VMEM((4, LANES), f32),
            pltpu.VMEM((OWN, LANES), f32),
            pltpu.VMEM(cc.shape, f32),
            pltpu.VMEM(cq.shape, f32),
            pltpu.VMEM((levels, SLOTS, LANES), i32),
            pltpu.VMEM((levels, SLOTS, LANES), i32),
            pltpu.VMEM((3, 512, LANES), f32),
            pltpu.VMEM((3, 512, LANES), f32),
            pltpu.VMEM((levels, 8, LANES), i32),
            pltpu.VMEM((levels - 1, SLOTS, LANES), i32),
            pltpu.VMEM((levels - 1, SLOTS, LANES), i32),
            pltpu.VMEM((levels, 10, 8, LANES), f32),
            pltpu.VMEM((levels, BLOCK, LANES), f32),
            pltpu.VMEM((OWN * COMPS + levels * BLOCK, LANES), f32),
            pltpu.VMEM((2, 16, LANES), f32),
            pltpu.VMEM((2, 16, LANES), f32),
            dma((7,)),
            dma((levels,)),
            dma((levels,)),
            dma((levels - 1,)),
            dma((levels - 1,)),
            dma((2,)),
            dma((2,)),
        ],
        compiler_params=pltpu.CompilerParams(collective_id=0, has_side_effects=True),
        name="treecode",
    )(
        pos,
        mass.reshape(4, LANES),
        cm.reshape(OWN, LANES),
        cc,
        cq,
        lists.reshape(levels, SLOTS, LANES),
        masks.reshape(levels, SLOTS, LANES),
        face_lists,
        face_counts,
    )


def solution(mesh):
    sizes = tuple(mesh.shape[a] for a in AXES)
    in_specs = (
        P(None, AXES),
        P(AXES),
        P(AXES),
        P(None, AXES),
        P(None, AXES),
        P(AXES, None, None),
        P(AXES, None, None),
        P(AXES, None, None),
        P(AXES, None),
    )
    return jax.shard_map(
        functools.partial(shards, sizes),
        mesh=mesh,
        in_specs=in_specs,
        out_specs=P(None, AXES),
        check_vma=False,
    )
```

```python
import functools

import jax
import jax.numpy as jnp
from jax import lax
from jax.experimental import pallas as pl
from jax.experimental.pallas import tpu as pltpu
from jax.sharding import PartitionSpec as P

MESH = pl.DeviceIdType.MESH
AXES = ("gx", "gy", "gz")
SOFTEN = 0.01
LANES = 128
OWN = 2048 // LANES
SLOTS = 1024 // LANES
LIVE = 768 // LANES
COMPS = 10
BLOCK = 64
GROUP = 32
KEEP = 8192
STEPS = ((0, 1), (2,), (3,), (4,))
BODIES = 2
PLAN = (
    (8, 7, 2, 0),
    (8, 8, 4, 1),
    (11, 10, 6, 3),
    (15, 12, 8, 6),
    (20, 20, 12, 10),
)


def row8(row):
    return jnp.broadcast_to(row, (8, LANES))


def flipped(value, bit):
    unit = 2**bit
    return value + unit - 2 * unit * lax.rem(lax.div(value, unit), 2)


def kernel(
    sizes,
    levels,
    pos_h,
    mass_h,
    cm_h,
    cc_h,
    cq_h,
    lists_h,
    masks_h,
    face_lists,
    face_counts,
    out_ref,
    pos,
    mass,
    cm,
    cc,
    cq,
    lists,
    masks,
    xb,
    acc,
    slot_ids,
    ranks,
    their_ranks,
    part,
    sent,
    table,
    bodies_out,
    bodies_in,
    in_sem,
    send_sem,
    recv_sem,
    rank_send_sem,
    rank_recv_sem,
    body_send_sem,
    body_recv_sem,
    far_cells,
    far_ranks,
    near_ids,
    ids_out,
    far_send_sem,
    far_recv_sem,
):
    nx, ny, nz = sizes
    bz, by = nz.bit_length() - 1, ny.bit_length() - 1
    bits = nx.bit_length() - 1 + by + bz
    gx, gy, gz = (lax.axis_index(a) for a in AXES)

    loads = {}
    for n, (name, src, dst) in enumerate(
        (
            ("lists", lists_h, lists),
            ("masks", masks_h, masks),
            ("cm", cm_h, cm),
            ("cc", cc_h, cc),
            ("cq", cq_h, cq),
            ("pos", pos_h, pos),
            ("mass", mass_h, mass),
        )
    ):
        loads[name] = pltpu.make_async_copy(src, dst, in_sem.at[n])
        loads[name].start()

    def across(at, level):
        bit = bits - 1 - level
        if bit >= by + bz:
            return (flipped(at[0], bit - by - bz), at[1], at[2])
        if bit >= bz:
            return (at[0], flipped(at[1], bit - bz), at[2])
        return (at[0], at[1], flipped(at[2], bit))

    partners = [across((gx, gy, gz), level) for level in range(levels)]
    joined = [step for step in STEPS if len(step) == 2]
    far_peers = [across(partners[step[0]], step[1]) for step in joined]
    lower = (gx, gy, lax.rem(gz + nz - 1, nz))
    upper = (gx, gy, lax.rem(gz + 1, nz))
    barrier = pltpu.get_barrier_semaphore()
    for peer in partners + far_peers + [lower, upper]:
        pl.semaphore_signal(barrier, inc=1, device_id=peer, device_id_type=MESH)

    late = lax.rem(gx, 2) * 2 + lax.div(gy, 4)
    others = lax.div((gx * ny + gy) * nz + gz + nx * ny * nz - 1, nx * ny * nz)
    late = late + 3 * (1 - others)
    steps = [lax.div(late + 3, 4), lax.div(late + 2, 4), lax.div(late + 1, 4)]

    def bound(window):
        b = PLAN[window]
        return b[0] + sum((b[i + 1] - b[i]) * steps[i] for i in range(3))

    loads["lists"].wait()
    loads["masks"].wait()
    lane = lax.broadcasted_iota(jnp.int32, (8, LANES), 1)
    slot = lax.broadcasted_iota(jnp.int32, (8, LANES), 0) * LANES + lane

    def dot(x, y):
        return jnp.dot(x, y, preferred_element_type=jnp.float32)

    def square(n, test):
        i = lax.broadcasted_iota(jnp.int32, (n, n), 0)
        j = lax.broadcasted_iota(jnp.int32, (n, n), 1)
        return test(i, j).astype(jnp.float32)

    stacked = jnp.concatenate([masks[level] for level in range(levels)], axis=0)
    stacked = stacked.astype(jnp.float32)
    before = dot(stacked, square(LANES, lambda i, j: i < j))
    totals = dot(stacked, jnp.ones((LANES, LANES), jnp.float32))
    base = dot(square(8 * levels, lambda i, j: ((i >> 3) == (j >> 3)) & (i > j)), totals)
    rank = (before + base).astype(jnp.int32)
    packed = []
    for level in range(levels):
        place = rank[8 * level : 8 * level + 8]
        on = masks[level] > 0
        if level < levels - 1:
            ranks[level] = jnp.where(on, place, -1)
        packed.append(jnp.where(on, lists[level] + (slot - place) * KEEP, 0))
    shift = 1
    while shift <= (SLOTS - LIVE) * LANES:
        flag = shift * KEEP
        for level in range(levels):
            w = packed[level]
            if shift < LANES:
                turned = pltpu.roll(w, LANES - shift, 1)
                coming = jnp.where(lane < LANES - shift, turned, pltpu.roll(turned, 7, 0))
            else:
                coming = pltpu.roll(w, 8 - shift // LANES, 0)
            coming = jnp.where(slot < SLOTS * LANES - shift, coming, 0)
            stay = jnp.where((w & flag) != 0, 0, w)
            packed[level] = jnp.where((coming & flag) != 0, coming, stay)
        shift *= 2
    for level in range(levels):
        slot_ids[level] = jnp.where(slot < LIVE * LANES, packed[level] & (KEEP - 1), -1)
    for n, step in enumerate(joined):
        ids_out[n] = slot_ids[step[1]]

    def level_start(level):
        return OWN * COMPS + BLOCK * level

    def own_row(c, k):
        return table[pl.ds(k * COMPS + c, 1), :]

    def got_row(level):
        return lambda c, k: table[pl.ds(level_start(level) + k * COMPS + c, 1), :]

    def pick_own(level):
        ids = slot_ids[level]
        rows, cols = ids >> 7, ids & (LANES - 1)

        def step(k, found):
            here = rows == k
            return tuple(
                jnp.where(here, jnp.take_along_axis(row8(own_row(c, k)), cols, axis=1), found[c])
                for c in range(10)
            )

        found = tuple(jnp.zeros((8, LANES), jnp.float32) for _ in range(10))
        found = lax.fori_loop(0, OWN, step, found, unroll=8)
        return list(found)

    def pick_got(level, source, found):
        ids = slot_ids[level]
        rows, cols = ids >> 7, ids & (LANES - 1)
        for k in range(LIVE):
            here = rows == OWN + source * SLOTS + k
            for c in range(10):
                row = row8(got_row(source)(c, k))
                found[c] = jnp.where(here, jnp.take_along_axis(row, cols, axis=1), found[c])
        return found

    def placed(ids, source, table_of_ranks):
        rows, cols = ids >> 7, ids & (LANES - 1)
        first = OWN + source * SLOTS
        place = ids
        for k in range(SLOTS):
            row = row8(table_of_ranks[k : k + 1, :])
            value = jnp.take_along_axis(row, cols, axis=1)
            value = jnp.where(value < 0, -1, value + first * LANES)
            place = jnp.where(rows == first + k, value, place)
        return place

    def translate(level, source):
        slot_ids[level] = placed(slot_ids[level], source, their_ranks.at[source])

    def finish(n):
        a, b = joined[n]
        ids = placed(near_ids[n], a, far_ranks.at[n])
        rows, cols = ids >> 7, ids & (LANES - 1)
        here = [rows == OWN + a * SLOTS + k for k in range(LIVE)]
        copies[b].wait_recv()
        far_copies[n].wait_recv()
        pad = jnp.zeros((8 - LIVE, LANES), jnp.float32)
        for c in range(COMPS):
            spots = pl.ds(level_start(b) + c, LIVE, stride=COMPS)
            value = jnp.concatenate([table[spots, :], pad], axis=0)
            for k in range(LIVE):
                row = row8(far_cells[n, k * COMPS + c : k * COMPS + c + 1, :])
                value = jnp.where(here[k], jnp.take_along_axis(row, cols, axis=1), value)
            table[spots, :] = value[:LIVE]

    def stage(level, found):
        for c in range(COMPS):
            sent[level, pl.ds(c, LIVE, stride=COMPS), :] = found[c][:LIVE]

    def send(level, found):
        stage(level, found)
        copies[level].start()

    copies = [
        pltpu.make_async_remote_copy(
            src_ref=sent.at[level],
            dst_ref=table.at[pl.ds(level_start(level), BLOCK)],
            send_sem=send_sem.at[level],
            recv_sem=recv_sem.at[level],
            device_id=partners[level],
            device_id_type=MESH,
        )
        for level in range(levels)
    ]
    rank_copies = [
        pltpu.make_async_remote_copy(
            src_ref=ranks.at[level],
            dst_ref=their_ranks.at[level],
            send_sem=rank_send_sem.at[level],
            recv_sem=rank_recv_sem.at[level],
            device_id=partners[level],
            device_id_type=MESH,
        )
        for level in range(levels - 1)
    ]
    far_copies, far_small = [], []
    for n, step in enumerate(joined):
        for which, (src, dst, peer) in enumerate(
            (
                (sent.at[step[0]], far_cells.at[n], far_peers[n]),
                (ranks.at[step[0]], far_ranks.at[n], far_peers[n]),
                (ids_out.at[n], near_ids.at[n], partners[step[1]]),
            )
        ):
            copy = pltpu.make_async_remote_copy(
                src_ref=src,
                dst_ref=dst,
                send_sem=far_send_sem.at[n, which],
                recv_sem=far_recv_sem.at[n, which],
                device_id=peer,
                device_id_type=MESH,
            )
            if which == 0:
                far_copies.append(copy)
            else:
                far_small.append(copy)
    body_copies = [
        pltpu.make_async_remote_copy(
            src_ref=bodies_out.at[side],
            dst_ref=bodies_in.at[1 - side],
            send_sem=body_send_sem.at[side],
            recv_sem=body_recv_sem.at[1 - side],
            device_id=peer,
            device_id_type=MESH,
        )
        for side, peer in enumerate((lower, upper))
    ]

    loads["cm"].wait()
    loads["cc"].wait()
    loads["cq"].wait()
    for k in range(OWN):
        cols = slice(k * LANES, (k + 1) * LANES)
        table[k * COMPS : k * COMPS + 1, :] = cm[k : k + 1, :]
        table[k * COMPS + 1 : k * COMPS + 4, :] = cc[:, cols]
        table[k * COMPS + 4 : (k + 1) * COMPS, :] = cq[:, cols]
    stage(0, pick_own(0))
    loads["pos"].wait()
    loads["mass"].wait()

    def pack_bodies():
        for side in range(2):
            for block in range(4):
                listed = jnp.int32(0)
                for j in range(4):
                    hit = (face_lists[0, side, j] == block) & (j < face_counts[0, side])
                    listed = listed + hit.astype(jnp.int32)
                kept_mass = jnp.where(listed > 0, mass[block : block + 1, :], 0.0)
                bodies_out[side, block : block + 1, :] = kept_mass
            for a in range(3):
                for block in range(4):
                    bodies_out[side, 4 + 4 * a + block : 5 + 4 * a + block, :] = pos[
                        a : a + 1, block * LANES : (block + 1) * LANES
                    ]

    def spread():
        for a in range(3):
            for block in range(4):
                row = pos[a : a + 1, block * LANES : (block + 1) * LANES]
                xb[a, block * LANES : (block + 1) * LANES, :] = jnp.broadcast_to(
                    row, (LANES, LANES)
                ).T
        acc[...] = jnp.zeros_like(acc)

    def cells_step(read, units, at):
        x = [xb[a, pl.ds(at, GROUP), :] for a in range(3)]
        total = [acc[a, pl.ds(at, GROUP), :] for a in range(3)]
        for k in units:
            m, c0, c1, c2, xx, yy, zz, xy, xz, yz = (read(c, k) for c in range(COMPS))
            d0, d1, d2 = x[0] - c0, x[1] - c1, x[2] - c2
            s = (d0 * d0 + d1 * d1) + (d2 * d2 + SOFTEN)
            u = lax.rsqrt(s)
            u2 = u * u
            q0 = xx * d0 + xy * d1 + xz * d2
            q1 = xy * d0 + yy * d1 + yz * d2
            q2 = xz * d0 + yz * d1 + zz * d2
            form = d0 * q0 + d1 * q1 + d2 * q2
            u5 = u2 * u2 * u
            w = m * s + 2.5 * (form * u2)
            total[0] = total[0] + u5 * (q0 - w * d0)
            total[1] = total[1] + u5 * (q1 - w * d1)
            total[2] = total[2] + u5 * (q2 - w * d2)
        for a in range(3):
            acc[a, pl.ds(at, GROUP), :] = total[a]

    def add_pairs(lo, hi):
        def pair(p, _):
            level = lax.div(jnp.maximum(p - 8, 0), 3)
            start = 2 * COMPS * p + (BLOCK - LIVE * COMPS) * level

            def step(g, _):
                cells_step(
                    lambda c, k: table[pl.ds(start + COMPS * k + c, 1), :],
                    range(2),
                    pl.multiple_of(g * GROUP, GROUP),
                )
                return 0

            return lax.fori_loop(0, 512 // GROUP, step, 0)

        lax.fori_loop(lo, hi, pair, 0)

    def add_bodies(read, rows):
        def step(g, _):
            at = pl.multiple_of(g * GROUP, GROUP)
            x = [xb[a, pl.ds(at, GROUP), :] for a in range(3)]
            total = [acc[a, pl.ds(at, GROUP), :] for a in range(3)]
            for k in rows:
                m, c0, c1, c2 = (read(c, k) for c in range(4))
                d0, d1, d2 = x[0] - c0, x[1] - c1, x[2] - c2
                s = (d0 * d0 + d1 * d1) + (d2 * d2 + SOFTEN)
                u = lax.rsqrt(s)
                p = m * (u * u * u)
                total[0] = total[0] - p * d0
                total[1] = total[1] - p * d1
                total[2] = total[2] - p * d2
            for a in range(3):
                acc[a, pl.ds(at, GROUP), :] = total[a]
            return 0

        lax.fori_loop(0, 512 // GROUP, step, 0)

    def own_bodies(c, k):
        if c == 0:
            return mass[k : k + 1, :]
        return pos[c - 1 : c, k * LANES : (k + 1) * LANES]

    def near(side):
        body_copies[1 - side].wait_recv()
        inside = (gz > 0) if side == 0 else (gz < nz - 1)

        @pl.when(inside)
        def _():
            add_bodies(lambda c, k: bodies_in[side, 4 * c + k : 4 * c + k + 1, :], range(4))

    def keep(level, found):
        for c in range(10):
            part[level, c] = found[c]

    def kept(level):
        return [part[level, c] for c in range(10)]

    early = late < 3

    @pl.when(early)
    def _():
        spread()
        add_pairs(0, bound(0))

    pl.semaphore_wait(barrier, levels + 2 + len(joined))
    copies[0].start()
    far = dict((step[0], n) for n, step in enumerate(joined))
    if 0 in far:
        far_copies[0].start()
    for copy in rank_copies + far_small:
        copy.start()
    if 0 in far:
        send(1, pick_own(1))
    pack_bodies()
    for copy in body_copies:
        copy.start()

    @pl.when(jnp.logical_not(early))
    def _():
        spread()

    known = []
    for i, step in enumerate(STEPS):
        for level in STEPS[i + 1] if i + 1 < len(STEPS) else ():
            found = pick_own(level)
            for source in known:
                found = pick_got(level, source, found)
            keep(level, found)
        if i == BODIES:
            add_bodies(own_bodies, range(4))
            near(0)
            near(1)
        add_pairs(bound(i), bound(i + 1))
        n = far.get(step[0])
        last = step[-1] == levels - 1
        for level in step:
            if level < levels - 1:
                rank_copies[level].wait_recv()
                for later in range(step[-1] + 1, levels):
                    translate(later, level)
        if n is not None:
            far_small[2 * n].wait_recv()
            far_small[2 * n + 1].wait_recv()
            if last:
                copies[step[0]].wait_recv()
                add_pairs(bound(i + 1), 8 + 3 * (levels - 1))
            finish(n)
        if last:
            if n is None:
                copies[step[0]].wait_recv()
                add_pairs(bound(i + 1), 8 + 3 * (levels - 1))
            break
        sources = [step[1]] if n is not None else []
        ahead = STEPS[i + 1]
        found = kept(ahead[0])
        for source in sources:
            found = pick_got(ahead[0], source, found)
        copies[step[0]].wait_recv()
        send(ahead[0], pick_got(ahead[0], step[0], found))
        if ahead[0] in far:
            far_copies[far[ahead[0]]].start()
        for later in ahead[1:]:
            found = kept(later)
            for source in step:
                found = pick_got(later, source, found)
            send(later, found)
        known += list(step)
    for block in range(4):
        for g in range(LANES // GROUP):
            cells_step(got_row(levels - 1), range(LIVE), block * LANES + g * GROUP)
        for a in range(3):
            turned = acc[a, block * LANES : (block + 1) * LANES, :].T
            out_ref[a : a + 1, block * LANES : (block + 1) * LANES] = jnp.sum(
                turned, axis=0, keepdims=True
            )
    for copy in copies + rank_copies + far_copies + far_small + body_copies:
        copy.wait_send()


def shards(sizes, pos, mass, cm, cc, cq, lists, masks, face_lists, face_counts):
    levels = lists.shape[1]
    joined = sum(len(step) == 2 for step in STEPS)
    f32, i32 = jnp.float32, jnp.int32
    any_space = pl.BlockSpec(memory_space=pl.ANY)
    smem = pl.BlockSpec(memory_space=pltpu.SMEM)
    dma = pltpu.SemaphoreType.DMA
    return pl.pallas_call(
        functools.partial(kernel, sizes, levels),
        out_shape=pltpu.VMEM(pos.shape, f32),
        in_specs=[any_space] * 7 + [smem] * 2,
        out_specs=pl.BlockSpec(memory_space=pltpu.VMEM),
        scratch_shapes=[
            pltpu.VMEM(pos.shape, f32),
            pltpu.VMEM((4, LANES), f32),
            pltpu.VMEM((OWN, LANES), f32),
            pltpu.VMEM(cc.shape, f32),
            pltpu.VMEM(cq.shape, f32),
            pltpu.VMEM((levels, SLOTS, LANES), i32),
            pltpu.VMEM((levels, SLOTS, LANES), i32),
            pltpu.VMEM((3, 512, LANES), f32),
            pltpu.VMEM((3, 512, LANES), f32),
            pltpu.VMEM((levels, 8, LANES), i32),
            pltpu.VMEM((levels - 1, SLOTS, LANES), i32),
            pltpu.VMEM((levels - 1, SLOTS, LANES), i32),
            pltpu.VMEM((levels, 10, 8, LANES), f32),
            pltpu.VMEM((levels, BLOCK, LANES), f32),
            pltpu.VMEM((OWN * COMPS + levels * BLOCK, LANES), f32),
            pltpu.VMEM((2, 16, LANES), f32),
            pltpu.VMEM((2, 16, LANES), f32),
            dma((7,)),
            dma((levels,)),
            dma((levels,)),
            dma((levels - 1,)),
            dma((levels - 1,)),
            dma((2,)),
            dma((2,)),
            pltpu.VMEM((joined, BLOCK, LANES), f32),
            pltpu.VMEM((joined, SLOTS, LANES), i32),
            pltpu.VMEM((joined, 8, LANES), i32),
            pltpu.VMEM((joined, 8, LANES), i32),
            dma((joined, 3)),
            dma((joined, 3)),
        ],
        compiler_params=pltpu.CompilerParams(collective_id=0, has_side_effects=True),
        name="treecode",
    )(
        pos,
        mass.reshape(4, LANES),
        cm.reshape(OWN, LANES),
        cc,
        cq,
        lists.reshape(levels, SLOTS, LANES),
        masks.reshape(levels, SLOTS, LANES),
        face_lists,
        face_counts,
    )


def solution(mesh):
    sizes = tuple(mesh.shape[a] for a in AXES)
    in_specs = (
        P(None, AXES),
        P(AXES),
        P(AXES),
        P(None, AXES),
        P(None, AXES),
        P(AXES, None, None),
        P(AXES, None, None),
        P(AXES, None, None),
        P(AXES, None),
    )
    return jax.shard_map(
        functools.partial(shards, sizes),
        mesh=mesh,
        in_specs=in_specs,
        out_specs=P(None, AXES),
        check_vma=False,
    )
```

```python
import functools

import jax
import jax.numpy as jnp
from jax import lax
from jax.experimental import pallas as pl
from jax.experimental.pallas import tpu as pltpu
from jax.sharding import PartitionSpec as P

MESH = pl.DeviceIdType.MESH
AXES = ("gx", "gy", "gz")
SOFTEN = 0.01
LANES = 128
OWN = 2048 // LANES
SLOTS = 1024 // LANES
LIVE = 768 // LANES
COMPS = 10
BLOCK = 64
GROUP = 32
KEEP = 8192
STEPS = ((0, 1), (2, 3), (4,))
PLAN = (
    (8, 7, 2, 0),
    (8, 8, 4, 2),
    (14, 11, 7, 6),
    (20, 20, 13, 11),
)


def row8(row):
    return jnp.broadcast_to(row, (8, LANES))


def flipped(value, bit):
    unit = 2**bit
    return value + unit - 2 * unit * lax.rem(lax.div(value, unit), 2)


def kernel(
    sizes,
    levels,
    pos_h,
    mass_h,
    cm_h,
    cc_h,
    cq_h,
    lists_h,
    masks_h,
    face_lists,
    face_counts,
    out_ref,
    pos,
    mass,
    cm,
    cc,
    cq,
    lists,
    masks,
    xb,
    acc,
    slot_ids,
    ranks,
    their_ranks,
    part,
    sent,
    table,
    bodies_out,
    bodies_in,
    in_sem,
    send_sem,
    recv_sem,
    rank_send_sem,
    rank_recv_sem,
    body_send_sem,
    body_recv_sem,
    far_cells,
    far_ranks,
    near_ids,
    ids_out,
    far_send_sem,
    far_recv_sem,
):
    nx, ny, nz = sizes
    bz, by = nz.bit_length() - 1, ny.bit_length() - 1
    bits = nx.bit_length() - 1 + by + bz
    gx, gy, gz = (lax.axis_index(a) for a in AXES)

    loads = {}
    for n, (name, src, dst) in enumerate(
        (
            ("lists", lists_h, lists),
            ("masks", masks_h, masks),
            ("cm", cm_h, cm),
            ("cc", cc_h, cc),
            ("cq", cq_h, cq),
            ("pos", pos_h, pos),
            ("mass", mass_h, mass),
        )
    ):
        loads[name] = pltpu.make_async_copy(src, dst, in_sem.at[n])
        loads[name].start()

    def across(at, level):
        bit = bits - 1 - level
        if bit >= by + bz:
            return (flipped(at[0], bit - by - bz), at[1], at[2])
        if bit >= bz:
            return (at[0], flipped(at[1], bit - bz), at[2])
        return (at[0], at[1], flipped(at[2], bit))

    partners = [across((gx, gy, gz), level) for level in range(levels)]
    joined = [step for step in STEPS if len(step) == 2]
    far_peers = [across(partners[step[0]], step[1]) for step in joined]
    lower = (gx, gy, lax.rem(gz + nz - 1, nz))
    upper = (gx, gy, lax.rem(gz + 1, nz))
    barrier = pltpu.get_barrier_semaphore()
    for peer in partners + far_peers + [lower, upper]:
        pl.semaphore_signal(barrier, inc=1, device_id=peer, device_id_type=MESH)

    late = lax.rem(gx, 2) * 2 + lax.div(gy, 4)
    others = lax.div((gx * ny + gy) * nz + gz + nx * ny * nz - 1, nx * ny * nz)
    late = late + 3 * (1 - others)
    steps = [lax.div(late + 3, 4), lax.div(late + 2, 4), lax.div(late + 1, 4)]

    def bound(window):
        b = PLAN[window]
        return b[0] + sum((b[i + 1] - b[i]) * steps[i] for i in range(3))

    loads["lists"].wait()
    loads["masks"].wait()
    lane = lax.broadcasted_iota(jnp.int32, (8, LANES), 1)
    slot = lax.broadcasted_iota(jnp.int32, (8, LANES), 0) * LANES + lane

    def dot(x, y):
        return jnp.dot(x, y, preferred_element_type=jnp.float32)

    def square(n, test):
        i = lax.broadcasted_iota(jnp.int32, (n, n), 0)
        j = lax.broadcasted_iota(jnp.int32, (n, n), 1)
        return test(i, j).astype(jnp.float32)

    stacked = jnp.concatenate([masks[level] for level in range(levels)], axis=0)
    stacked = stacked.astype(jnp.float32)
    before = dot(stacked, square(LANES, lambda i, j: i < j))
    totals = dot(stacked, jnp.ones((LANES, LANES), jnp.float32))
    base = dot(square(8 * levels, lambda i, j: ((i >> 3) == (j >> 3)) & (i > j)), totals)
    rank = (before + base).astype(jnp.int32)
    packed = []
    for level in range(levels):
        place = rank[8 * level : 8 * level + 8]
        on = masks[level] > 0
        if level < levels - 1:
            ranks[level] = jnp.where(on, place, -1)
        packed.append(jnp.where(on, lists[level] + (slot - place) * KEEP, 0))
    shift = 1
    while shift <= (SLOTS - LIVE) * LANES:
        flag = shift * KEEP
        for level in range(levels):
            w = packed[level]
            if shift < LANES:
                turned = pltpu.roll(w, LANES - shift, 1)
                coming = jnp.where(lane < LANES - shift, turned, pltpu.roll(turned, 7, 0))
            else:
                coming = pltpu.roll(w, 8 - shift // LANES, 0)
            coming = jnp.where(slot < SLOTS * LANES - shift, coming, 0)
            stay = jnp.where((w & flag) != 0, 0, w)
            packed[level] = jnp.where((coming & flag) != 0, coming, stay)
        shift *= 2
    for level in range(levels):
        slot_ids[level] = jnp.where(slot < LIVE * LANES, packed[level] & (KEEP - 1), -1)
    for n, step in enumerate(joined):
        ids_out[n] = slot_ids[step[1]]

    def level_start(level):
        return OWN * COMPS + BLOCK * level

    def own_row(c, k):
        return table[pl.ds(k * COMPS + c, 1), :]

    def got_row(level):
        return lambda c, k: table[pl.ds(level_start(level) + k * COMPS + c, 1), :]

    def pick_own(level):
        ids = slot_ids[level]
        rows, cols = ids >> 7, ids & (LANES - 1)

        def step(k, found):
            here = rows == k
            return tuple(
                jnp.where(here, jnp.take_along_axis(row8(own_row(c, k)), cols, axis=1), found[c])
                for c in range(10)
            )

        found = tuple(jnp.zeros((8, LANES), jnp.float32) for _ in range(10))
        found = lax.fori_loop(0, OWN, step, found, unroll=8)
        return list(found)

    def pick_got(level, source, found):
        ids = slot_ids[level]
        rows, cols = ids >> 7, ids & (LANES - 1)
        for k in range(LIVE):
            here = rows == OWN + source * SLOTS + k
            for c in range(10):
                row = row8(got_row(source)(c, k))
                found[c] = jnp.where(here, jnp.take_along_axis(row, cols, axis=1), found[c])
        return found

    def placed(ids, source, table_of_ranks):
        rows, cols = ids >> 7, ids & (LANES - 1)
        first = OWN + source * SLOTS
        place = ids
        for k in range(SLOTS):
            row = row8(table_of_ranks[k : k + 1, :])
            value = jnp.take_along_axis(row, cols, axis=1)
            value = jnp.where(value < 0, -1, value + first * LANES)
            place = jnp.where(rows == first + k, value, place)
        return place

    def translate(level, source):
        slot_ids[level] = placed(slot_ids[level], source, their_ranks.at[source])

    def finish(n):
        a, b = joined[n]
        ids = placed(near_ids[n], a, far_ranks.at[n])
        rows, cols = ids >> 7, ids & (LANES - 1)
        here = [rows == OWN + a * SLOTS + k for k in range(LIVE)]
        copies[b].wait_recv()
        far_copies[n].wait_recv()
        pad = jnp.zeros((8 - LIVE, LANES), jnp.float32)
        for c in range(COMPS):
            spots = pl.ds(level_start(b) + c, LIVE, stride=COMPS)
            value = jnp.concatenate([table[spots, :], pad], axis=0)
            for k in range(LIVE):
                row = row8(far_cells[n, k * COMPS + c : k * COMPS + c + 1, :])
                value = jnp.where(here[k], jnp.take_along_axis(row, cols, axis=1), value)
            table[spots, :] = value[:LIVE]

    def stage(level, found):
        for c in range(COMPS):
            sent[level, pl.ds(c, LIVE, stride=COMPS), :] = found[c][:LIVE]

    def send(level, found):
        stage(level, found)
        copies[level].start()

    copies = [
        pltpu.make_async_remote_copy(
            src_ref=sent.at[level],
            dst_ref=table.at[pl.ds(level_start(level), BLOCK)],
            send_sem=send_sem.at[level],
            recv_sem=recv_sem.at[level],
            device_id=partners[level],
            device_id_type=MESH,
        )
        for level in range(levels)
    ]
    rank_copies = [
        pltpu.make_async_remote_copy(
            src_ref=ranks.at[level],
            dst_ref=their_ranks.at[level],
            send_sem=rank_send_sem.at[level],
            recv_sem=rank_recv_sem.at[level],
            device_id=partners[level],
            device_id_type=MESH,
        )
        for level in range(levels - 1)
    ]
    far_copies, far_small = [], []
    for n, step in enumerate(joined):
        for which, (src, dst, peer) in enumerate(
            (
                (sent.at[step[0]], far_cells.at[n], far_peers[n]),
                (ranks.at[step[0]], far_ranks.at[n], far_peers[n]),
                (ids_out.at[n], near_ids.at[n], partners[step[1]]),
            )
        ):
            copy = pltpu.make_async_remote_copy(
                src_ref=src,
                dst_ref=dst,
                send_sem=far_send_sem.at[n, which],
                recv_sem=far_recv_sem.at[n, which],
                device_id=peer,
                device_id_type=MESH,
            )
            if which == 0:
                far_copies.append(copy)
            else:
                far_small.append(copy)
    body_copies = [
        pltpu.make_async_remote_copy(
            src_ref=bodies_out.at[side],
            dst_ref=bodies_in.at[1 - side],
            send_sem=body_send_sem.at[side],
            recv_sem=body_recv_sem.at[1 - side],
            device_id=peer,
            device_id_type=MESH,
        )
        for side, peer in enumerate((lower, upper))
    ]

    loads["cm"].wait()
    loads["cc"].wait()
    loads["cq"].wait()
    for k in range(OWN):
        cols = slice(k * LANES, (k + 1) * LANES)
        table[k * COMPS : k * COMPS + 1, :] = cm[k : k + 1, :]
        table[k * COMPS + 1 : k * COMPS + 4, :] = cc[:, cols]
        table[k * COMPS + 4 : (k + 1) * COMPS, :] = cq[:, cols]
    stage(0, pick_own(0))
    loads["pos"].wait()
    loads["mass"].wait()

    def pack_bodies():
        for side in range(2):
            for block in range(4):
                listed = jnp.int32(0)
                for j in range(4):
                    hit = (face_lists[0, side, j] == block) & (j < face_counts[0, side])
                    listed = listed + hit.astype(jnp.int32)
                kept_mass = jnp.where(listed > 0, mass[block : block + 1, :], 0.0)
                bodies_out[side, block : block + 1, :] = kept_mass
            for a in range(3):
                for block in range(4):
                    bodies_out[side, 4 + 4 * a + block : 5 + 4 * a + block, :] = pos[
                        a : a + 1, block * LANES : (block + 1) * LANES
                    ]

    def spread():
        for a in range(3):
            for block in range(4):
                row = pos[a : a + 1, block * LANES : (block + 1) * LANES]
                xb[a, block * LANES : (block + 1) * LANES, :] = jnp.broadcast_to(
                    row, (LANES, LANES)
                ).T
        acc[...] = jnp.zeros_like(acc)

    def cells_step(read, units, at):
        x = [xb[a, pl.ds(at, GROUP), :] for a in range(3)]
        total = [acc[a, pl.ds(at, GROUP), :] for a in range(3)]
        for k in units:
            m, c0, c1, c2, xx, yy, zz, xy, xz, yz = (read(c, k) for c in range(COMPS))
            d0, d1, d2 = x[0] - c0, x[1] - c1, x[2] - c2
            s = (d0 * d0 + d1 * d1) + (d2 * d2 + SOFTEN)
            u = lax.rsqrt(s)
            u2 = u * u
            q0 = xx * d0 + xy * d1 + xz * d2
            q1 = xy * d0 + yy * d1 + yz * d2
            q2 = xz * d0 + yz * d1 + zz * d2
            form = d0 * q0 + d1 * q1 + d2 * q2
            u5 = u2 * u2 * u
            w = m * s + 2.5 * (form * u2)
            total[0] = total[0] + u5 * (q0 - w * d0)
            total[1] = total[1] + u5 * (q1 - w * d1)
            total[2] = total[2] + u5 * (q2 - w * d2)
        for a in range(3):
            acc[a, pl.ds(at, GROUP), :] = total[a]

    def add_pairs(lo, hi):
        def pair(p, _):
            level = lax.div(jnp.maximum(p - 8, 0), 3)
            start = 2 * COMPS * p + (BLOCK - LIVE * COMPS) * level

            def step(g, _):
                cells_step(
                    lambda c, k: table[pl.ds(start + COMPS * k + c, 1), :],
                    range(2),
                    pl.multiple_of(g * GROUP, GROUP),
                )
                return 0

            return lax.fori_loop(0, 512 // GROUP, step, 0)

        lax.fori_loop(lo, hi, pair, 0)

    def add_bodies(read, rows):
        def step(g, _):
            at = pl.multiple_of(g * GROUP, GROUP)
            x = [xb[a, pl.ds(at, GROUP), :] for a in range(3)]
            total = [acc[a, pl.ds(at, GROUP), :] for a in range(3)]
            for k in rows:
                m, c0, c1, c2 = (read(c, k) for c in range(4))
                d0, d1, d2 = x[0] - c0, x[1] - c1, x[2] - c2
                s = (d0 * d0 + d1 * d1) + (d2 * d2 + SOFTEN)
                u = lax.rsqrt(s)
                p = m * (u * u * u)
                total[0] = total[0] - p * d0
                total[1] = total[1] - p * d1
                total[2] = total[2] - p * d2
            for a in range(3):
                acc[a, pl.ds(at, GROUP), :] = total[a]
            return 0

        lax.fori_loop(0, 512 // GROUP, step, 0)

    def own_bodies(c, k):
        if c == 0:
            return mass[k : k + 1, :]
        return pos[c - 1 : c, k * LANES : (k + 1) * LANES]

    def near(side):
        body_copies[1 - side].wait_recv()
        inside = (gz > 0) if side == 0 else (gz < nz - 1)

        @pl.when(inside)
        def _():
            add_bodies(lambda c, k: bodies_in[side, 4 * c + k : 4 * c + k + 1, :], range(4))

    def keep(level, found):
        for c in range(10):
            part[level, c] = found[c]

    def kept(level):
        return [part[level, c] for c in range(10)]

    early = late < 3

    @pl.when(early)
    def _():
        spread()
        add_pairs(0, bound(0))

    pl.semaphore_wait(barrier, levels + 2 + len(joined))
    copies[0].start()
    far = dict((step[0], n) for n, step in enumerate(joined))
    if 0 in far:
        far_copies[0].start()
    for copy in rank_copies + far_small:
        copy.start()
    if 0 in far:
        send(1, pick_own(1))
    pack_bodies()
    for copy in body_copies:
        copy.start()

    @pl.when(jnp.logical_not(early))
    def _():
        spread()

    known = []
    for i, step in enumerate(STEPS):
        for level in STEPS[i + 1] if i + 1 < len(STEPS) else ():
            found = pick_own(level)
            for source in known:
                found = pick_got(level, source, found)
            keep(level, found)
        if i in (0, len(STEPS) - 1):
            @pl.when(late < 2 if i == 0 else late >= 2)
            def _():
                add_bodies(own_bodies, range(4))
                near(0)
                near(1)

        add_pairs(bound(i), bound(i + 1))
        n = far.get(step[0])
        last = step[-1] == levels - 1
        for level in step:
            if level < levels - 1:
                rank_copies[level].wait_recv()
                for later in range(step[-1] + 1, levels):
                    translate(later, level)
        if n is not None:
            far_small[2 * n].wait_recv()
            far_small[2 * n + 1].wait_recv()
            if last:
                copies[step[0]].wait_recv()
                add_pairs(bound(i + 1), 8 + 3 * (levels - 1))
            if step[0] > 0 and not last:
                copies[step[0]].wait_recv()
                soon = pick_got(STEPS[i + 1][0], step[0], kept(STEPS[i + 1][0]))
                finish(n)
            else:
                finish(n)
        if last:
            if n is None:
                copies[step[0]].wait_recv()
                add_pairs(bound(i + 1), 8 + 3 * (levels - 1))
            break
        sources = [step[1]] if n is not None else []
        ahead = STEPS[i + 1]
        if n is not None and step[0] > 0:
            send(ahead[0], pick_got(ahead[0], step[1], soon))
        else:
            found = kept(ahead[0])
            for source in sources:
                found = pick_got(ahead[0], source, found)
            copies[step[0]].wait_recv()
            send(ahead[0], pick_got(ahead[0], step[0], found))
        if ahead[0] in far:
            far_copies[far[ahead[0]]].start()
        for later in ahead[1:]:
            found = kept(later)
            for source in step:
                found = pick_got(later, source, found)
            send(later, found)
        known += list(step)
    for block in range(4):
        for g in range(LANES // GROUP):
            cells_step(got_row(levels - 1), range(LIVE), block * LANES + g * GROUP)
        for a in range(3):
            turned = acc[a, block * LANES : (block + 1) * LANES, :].T
            out_ref[a : a + 1, block * LANES : (block + 1) * LANES] = jnp.sum(
                turned, axis=0, keepdims=True
            )
    for copy in copies + rank_copies + far_copies + far_small + body_copies:
        copy.wait_send()


def shards(sizes, pos, mass, cm, cc, cq, lists, masks, face_lists, face_counts):
    levels = lists.shape[1]
    joined = sum(len(step) == 2 for step in STEPS)
    f32, i32 = jnp.float32, jnp.int32
    any_space = pl.BlockSpec(memory_space=pl.ANY)
    smem = pl.BlockSpec(memory_space=pltpu.SMEM)
    dma = pltpu.SemaphoreType.DMA
    return pl.pallas_call(
        functools.partial(kernel, sizes, levels),
        out_shape=pltpu.VMEM(pos.shape, f32),
        in_specs=[any_space] * 7 + [smem] * 2,
        out_specs=pl.BlockSpec(memory_space=pltpu.VMEM),
        scratch_shapes=[
            pltpu.VMEM(pos.shape, f32),
            pltpu.VMEM((4, LANES), f32),
            pltpu.VMEM((OWN, LANES), f32),
            pltpu.VMEM(cc.shape, f32),
            pltpu.VMEM(cq.shape, f32),
            pltpu.VMEM((levels, SLOTS, LANES), i32),
            pltpu.VMEM((levels, SLOTS, LANES), i32),
            pltpu.VMEM((3, 512, LANES), f32),
            pltpu.VMEM((3, 512, LANES), f32),
            pltpu.VMEM((levels, 8, LANES), i32),
            pltpu.VMEM((levels - 1, SLOTS, LANES), i32),
            pltpu.VMEM((levels - 1, SLOTS, LANES), i32),
            pltpu.VMEM((levels, 10, 8, LANES), f32),
            pltpu.VMEM((levels, BLOCK, LANES), f32),
            pltpu.VMEM((OWN * COMPS + levels * BLOCK, LANES), f32),
            pltpu.VMEM((2, 16, LANES), f32),
            pltpu.VMEM((2, 16, LANES), f32),
            dma((7,)),
            dma((levels,)),
            dma((levels,)),
            dma((levels - 1,)),
            dma((levels - 1,)),
            dma((2,)),
            dma((2,)),
            pltpu.VMEM((joined, BLOCK, LANES), f32),
            pltpu.VMEM((joined, SLOTS, LANES), i32),
            pltpu.VMEM((joined, 8, LANES), i32),
            pltpu.VMEM((joined, 8, LANES), i32),
            dma((joined, 3)),
            dma((joined, 3)),
        ],
        compiler_params=pltpu.CompilerParams(collective_id=0, has_side_effects=True),
        name="treecode",
    )(
        pos,
        mass.reshape(4, LANES),
        cm.reshape(OWN, LANES),
        cc,
        cq,
        lists.reshape(levels, SLOTS, LANES),
        masks.reshape(levels, SLOTS, LANES),
        face_lists,
        face_counts,
    )


def solution(mesh):
    sizes = tuple(mesh.shape[a] for a in AXES)
    in_specs = (
        P(None, AXES),
        P(AXES),
        P(AXES),
        P(None, AXES),
        P(None, AXES),
        P(AXES, None, None),
        P(AXES, None, None),
        P(AXES, None, None),
        P(AXES, None),
    )
    return jax.shard_map(
        functools.partial(shards, sizes),
        mesh=mesh,
        in_specs=in_specs,
        out_specs=P(None, AXES),
        check_vma=False,
    )
```
